32 devices in a mesh: expert: 8 (over y, x, core), group: 4 (over z).
Axes of the slice: x: 2, y: 2, z: 4, core: 2. Of those that a mesh axis runs over, the one named last changes fastest.
Arguments:
- tokens: bfloat16 [3840, 4096], P('expert', 'group'), may hold values from -6 to 6
- cotangent: bfloat16 [3840, 1024], P('expert'), may hold values from -6 to 6
- routing: int32 [3840, 1], P('expert'), may hold values from 0 to 7; in each aligned block of 480 rows (0 to 479, 480 to 959, ...) at most 120 rows name the same one
- stat_prev: float32 [8, 1024, 1024], P('expert', 'group'), as said below
- root_prev: bfloat16 [8, 1024, 1024], P('expert', 'group'), may hold values from -0.1875 to 0.1875
- owner_map: int32 [8], replicated, may hold values from 0 to 2, as said below
Outputs:
- statistic: float32 [8, 1024, 1024], P('expert', 'group')
- roots: bfloat16 [8, 1024, 1024], P('expert', 'group')
- update: bfloat16 [8, 4096, 1024], P('expert', 'group')
The draws below stay inside these ranges and needn't reach their ends.
Inputs may be any that keep to these rules, and one draw needn't show every extreme that they name: `routing`: in the rows of one device (aligned blocks of 480 rows) no expert is named more than 120 times, a bound that some block reaches. `owner_map`: A value below 2 names the index of expert that owns this expert's statistic; the value 2 marks a statistic that is not refreshed. Exactly 4 experts are refreshed; no owner holds more than 4 of them, and some owner holds exactly 4. `stat_prev`: each expert's block is symmetric and positive definite.
All inputs are finite; a program needn't handle non-finite values.
Results may differ from the reference program's by a relative error of at most 0.0055.
Values may be sent and summed in bfloat16 or wider, within the bound.
A program may use at most 64 MiB of HBM per device.

```python
import math
import jax
import jax.numpy as jnp
import numpy as np
from jax import lax

D = 4096
FF = 1024
TOK_DEV = 480
ITERS = 2
POWER = 8
EXPERTS = 8
CAP = 120
OWNERS = 2
MOST = 4
REFRESH = 4
TOKENS = 3840
N_EXPERT = 8


def draw_stat_prev(key, part):
    diag_key = jax.random.fold_in(key, 11)
    mix_key = jax.random.fold_in(key, 12)
    low_end, high_end = (math.log(0.3), math.log(3.0))
    diagonal = jnp.exp(jax.random.uniform(diag_key, (EXPERTS, FF), jnp.float32, low_end, high_end))
    mixing = jax.random.normal(mix_key, (EXPERTS, FF, FF), jnp.float32)
    gram = jnp.einsum('eij,ekj->eik', mixing, mixing, precision=lax.Precision.HIGHEST) / (2.0 * FF)
    gram = 0.5 * (gram + jnp.swapaxes(gram, 1, 2))
    identity = (lax.broadcasted_iota(jnp.int32, (FF, FF), 0) == lax.broadcasted_iota(jnp.int32, (FF, FF), 1)).astype(jnp.float32)
    return gram + diagonal[:, :, None] * identity[None, :, :]


def draw_owner_map(key, part):
    order_key = jax.random.fold_in(key, 21)
    star_key = jax.random.fold_in(key, 22)
    other_key = jax.random.fold_in(key, 23)
    others_count = max(OWNERS - 1, 1)
    order = jax.random.permutation(order_key, EXPERTS)
    star = jax.random.randint(star_key, (), 0, OWNERS)
    others = (star + 1 + jax.random.permutation(other_key, others_count)) % OWNERS
    ranks = jnp.arange(REFRESH, dtype=jnp.int32)
    picked = jnp.where(ranks < MOST, star, others[jnp.maximum(ranks - MOST, 0) % others_count])
    result = jnp.full((EXPERTS,), OWNERS, jnp.int32)
    return result.at[order[:REFRESH]].set(picked.astype(jnp.int32))


def block_scale(stream_key, extent, split, smallest, high):
    def one(dim, shards_of):
        heights = jax.random.uniform(jax.random.fold_in(jax.random.fold_in(stream_key, 6), dim), (shards_of,), jnp.float32, smallest / len(split), high / len(split))
        return jnp.repeat(jnp.exp(heights), extent[dim] // shards_of).reshape((-1,) + (1,) * (len(extent) - dim - 1))

    factor_of = one(*split[0])
    for cut in split[1:]:
        factor_of = factor_of * one(*cut)
    return factor_of


def deal_out(own_key, own, number, rows, count, top, limit, lean):
    order = jax.random.permutation(own_key, count)
    crowded, ordinary = portions_of(count, rows * top, limit, lean, True), portions_of(count, rows * top, limit, lean, False)
    places = jnp.arange(count)

    def named(lengths, offset_by):
        used = int((lengths > 0).sum())
        fixed = max(1, used // 4)
        shifted = fixed + (places - fixed + offset_by * (used - fixed)) % max(1, count - fixed)
        return jnp.zeros((count,), jnp.int32).at[order[jnp.where(places < fixed, places, shifted)]].set(jnp.asarray(lengths, jnp.int32))

    lengths = jnp.where(number % 4 == 0, named(crowded, number // 4), named(ordinary, number - number // 4 - 1))
    mixed = jax.random.permutation(jax.random.fold_in(own, 3), count)
    source_of, taker = mixed[0:count // 2 * 2:2], mixed[1:count // 2 * 2:2]
    slack = jnp.minimum(lengths[source_of] - 1, limit - lengths[taker]) // 2
    slack = jnp.where((source_of == order[0]) | (taker == order[0]) | (lengths[taker] == 0), 0, jnp.maximum(slack, 0))
    shifted = jax.random.randint(jax.random.fold_in(own, 4), (count // 2,), 0, 1 << 20) % (slack + 1)
    lengths = lengths.at[source_of].add(-shifted).at[taker].add(shifted)
    labels = jnp.searchsorted(jnp.cumsum(lengths), jnp.arange(rows * top), side="right").astype(jnp.int32)
    grid = labels.reshape(top, rows).T
    grid = grid[jax.random.permutation(jax.random.fold_in(own, 1), rows)]
    offset_by = jax.random.randint(jax.random.fold_in(own, 2), (rows, 1), 0, top)
    return jnp.take_along_axis(grid, (jnp.arange(top)[None, :] + offset_by) % top, axis=1)


def portions_of(number_of, total, bound, skew, full):
    portions = [(1 << 20) // math.isqrt(rank ** skew) + 1 for rank in range(1, number_of + 1)]
    largest = bound if full else min(bound, max(-(-total // number_of), total * portions[0] // sum(portions)))
    least = 1 if total - largest >= number_of - 1 else 0
    holding, surplus = [largest] + [least] * (number_of - 1), total - largest - least * (number_of - 1)
    while surplus > 0:
        candidates = [i for i in range(1, number_of) if holding[i] < largest] or [i for i in range(1, number_of) if holding[i] < bound]
        whole, remaining = sum([portions[i] for i in candidates]), surplus
        for i in candidates:
            more = min(bound - holding[i], max(1, remaining * portions[i] // whole), surplus)
            holding[i] = holding[i] + more
            surplus = surplus - more
    return np.array(holding)


def centred(own_key, shape, width, reach, pieces=(), kind=jnp.bfloat16):
    level = block_scale(own_key, shape, pieces, -0.22, 0.18) if pieces else 1.0
    values = jax.random.normal(own_key, shape, jnp.float32) * width * level
    return jnp.minimum(jnp.maximum(values, -reach), reach).astype(kind)


def setup_inputs(seed: int = 0) -> dict:
    keys = jax.random.split(jax.random.key(seed), 7)
    tokens = centred(keys[0], (TOKENS, D), 1.0, 6.0, ((0, 8), (1, 4)))
    cotangent = centred(keys[1], (TOKENS, FF), 1.0, 6.0, ((0, 8),))
    routing_keys = jax.random.split(jax.random.fold_in(keys[2], 1), TOKENS // TOK_DEV)
    routing_turns = jax.random.permutation(jax.random.fold_in(keys[2], 3), TOKENS // TOK_DEV)
    routing = jax.vmap(lambda own, number: deal_out(jax.random.fold_in(keys[2], 2), own, number, TOK_DEV, EXPERTS, 1, CAP, 2))(routing_keys, routing_turns).reshape((TOKENS, 1))
    stat_prev = draw_stat_prev(jax.random.fold_in(keys[6], 71), 0)
    root_prev = centred(keys[4], (EXPERTS, FF, FF), FF ** -0.5, 0.1875, ((0, 8), (1, 4)))
    owner_map = draw_owner_map(jax.random.fold_in(keys[6], 71), 0)
    return {"tokens": tokens, "cotangent": cotangent, "routing": routing, "stat_prev": stat_prev, "root_prev": root_prev, "owner_map": owner_map}


keep_share = 0.9

def newton_root(block):
    order = block.shape[0]
    vector = jnp.full((order,), 1.0 / math.sqrt(order), jnp.float32)
    length = jnp.ones((), jnp.float32)
    for turn_index in range(POWER):
        image = jnp.dot(block, vector.astype(jnp.bfloat16), preferred_element_type=jnp.float32)
        length = jnp.sqrt(jnp.sum(image * image))
        vector = image / length
    scaling = 2.5 / length
    identity = (lax.broadcasted_iota(jnp.int32, (order, order), 0) == lax.broadcasted_iota(jnp.int32, (order, order), 1)).astype(jnp.float32)
    moment = scaling * block.astype(jnp.float32)
    moment_low = moment.astype(jnp.bfloat16)
    iterate = identity
    for turn_index in range(ITERS):
        factor = ((5.0 * identity - moment) * 0.25).astype(jnp.bfloat16)
        if turn_index == 0:
            iterate = factor.astype(jnp.float32)
        else:
            iterate = jnp.dot(iterate.astype(jnp.bfloat16), factor, preferred_element_type=jnp.float32)
        if turn_index + 1 < ITERS:
            square = jnp.dot(factor, factor, preferred_element_type=jnp.float32).astype(jnp.bfloat16)
            fourth = jnp.dot(square, square, preferred_element_type=jnp.float32).astype(jnp.bfloat16)
            moment = jnp.dot(fourth, moment_low, preferred_element_type=jnp.float32)
            moment_low = moment.astype(jnp.bfloat16)
    return (jnp.sqrt(jnp.sqrt(scaling)) * iterate).astype(jnp.bfloat16)

def reference(tokens, cotangent, routing, stat_prev, root_prev, owner_map):
    total_rows = tokens.shape[0]
    route = routing[:, 0]
    expert_ids = jnp.arange(EXPERTS, dtype=jnp.int32)
    onehot = (route[:, None] == expert_ids[None, :]).astype(jnp.int32)
    running = jnp.cumsum(onehot.reshape(N_EXPERT, TOK_DEV, EXPERTS), axis=1).reshape(total_rows, EXPERTS)
    position = lax.optimization_barrier(jnp.sum(onehot * (running - 1), axis=1)).astype(jnp.int32)
    source = jnp.arange(total_rows, dtype=jnp.int32) // TOK_DEV
    column = (source * CAP + position).astype(jnp.int32)
    table = jnp.full((EXPERTS, N_EXPERT * CAP), total_rows, jnp.int32)
    table = table.at[route, column].set(jnp.arange(total_rows, dtype=jnp.int32))
    tokens_pad = jnp.concatenate([tokens, jnp.zeros((1, tokens.shape[1]), tokens.dtype)], 0)
    signal_pad = jnp.concatenate([cotangent, jnp.zeros((1, cotangent.shape[1]), cotangent.dtype)], 0)
    grad_scale = 1.0 / math.sqrt(TOK_DEV)

    def per_expert(inputs):
        rows, previous, prior_root, owner = inputs
        taken = tokens_pad[rows]
        signal = signal_pad[rows]
        grad = lax.dot_general(taken, signal, (((0,), (0,)), ((), ())), preferred_element_type=jnp.float32)
        grad = (grad * grad_scale).astype(jnp.bfloat16)
        gram = lax.dot_general(grad, grad, (((0,), (0,)), ((), ())), preferred_element_type=jnp.float32)
        statistic = keep_share * previous + (1.0 - keep_share) * gram / D
        root = lax.cond(owner < OWNERS, lambda: newton_root(statistic.astype(jnp.bfloat16)), lambda: prior_root)
        update = jnp.dot(grad, root, preferred_element_type=jnp.float32).astype(jnp.bfloat16)
        return (statistic, root, update)
    stats, roots, updates = lax.map(per_expert, (table, stat_prev, root_prev, owner_map))
    return (stats, roots, updates)
```

```python
import functools
import math

import jax
import jax.numpy as jnp
from jax import lax
from jax.experimental import pallas as pl
from jax.experimental.pallas import tpu as pltpu
from jax.sharding import PartitionSpec as P

ITERS = 2
POWER = 8
MESH = pl.DeviceIdType.MESH

keep_share = 0.9


def newton_root(block):
    order = block.shape[0]
    vector = jnp.full((order,), 1.0 / math.sqrt(order), jnp.float32)
    length = jnp.ones((), jnp.float32)
    for turn_index in range(POWER):
        image = jnp.dot(block, vector.astype(jnp.bfloat16), preferred_element_type=jnp.float32)
        length = jnp.sqrt(jnp.sum(image * image))
        vector = image / length
    scaling = 2.5 / length
    identity = (
        lax.broadcasted_iota(jnp.int32, (order, order), 0)
        == lax.broadcasted_iota(jnp.int32, (order, order), 1)
    ).astype(jnp.float32)
    moment = scaling * block.astype(jnp.float32)
    moment_low = moment.astype(jnp.bfloat16)
    iterate = identity
    for turn_index in range(ITERS):
        factor = ((5.0 * identity - moment) * 0.25).astype(jnp.bfloat16)
        if turn_index == 0:
            iterate = factor.astype(jnp.float32)
        else:
            iterate = jnp.dot(
                iterate.astype(jnp.bfloat16), factor, preferred_element_type=jnp.float32
            )
        if turn_index + 1 < ITERS:
            square = jnp.dot(factor, factor, preferred_element_type=jnp.float32).astype(
                jnp.bfloat16
            )
            fourth = jnp.dot(square, square, preferred_element_type=jnp.float32).astype(
                jnp.bfloat16
            )
            moment = jnp.dot(fourth, moment_low, preferred_element_type=jnp.float32)
            moment_low = moment.astype(jnp.bfloat16)
    return (jnp.sqrt(jnp.sqrt(scaling)) * iterate).astype(jnp.bfloat16)


def exchange_kernel(
    experts, groups, tok_ref, sig_ref, pay_ref, got_tok, got_sig, full,
    hold_tok, hold_sig, hold_pay, tok_send, tok_recv, sig_send, sig_recv, pay_send, pay_recv, own_sem,
):
    me = lax.axis_index("expert")
    mine = lax.axis_index("group")
    barrier = pltpu.get_barrier_semaphore()
    for d in range(1, experts):
        pl.semaphore_signal(
            barrier, inc=1, device_id={"expert": lax.rem(me + d, experts)}, device_id_type=MESH
        )
    for d in range(1, groups):
        pl.semaphore_signal(
            barrier, inc=1, device_id={"group": lax.rem(mine + d, groups)}, device_id_type=MESH
        )
    pl.semaphore_wait(barrier, experts + groups - 2)
    copies = []
    for d in range(1, max(experts, groups)):
        if d < groups:
            copies.append(
                pltpu.make_async_remote_copy(
                    src_ref=pay_ref,
                    dst_ref=full.at[mine],
                    send_sem=pay_send.at[d],
                    recv_sem=pay_recv.at[d],
                    device_id={"group": lax.rem(mine + d, groups)},
                    device_id_type=MESH,
                )
            )
        if d < experts:
            peer = lax.rem(me + d, experts)
            for src, dst, ssem, rsem in (
                (tok_ref, got_tok, tok_send, tok_recv),
                (sig_ref, got_sig, sig_send, sig_recv),
            ):
                copies.append(
                    pltpu.make_async_remote_copy(
                        src_ref=src.at[peer],
                        dst_ref=dst.at[me],
                        send_sem=ssem.at[d],
                        recv_sem=rsem.at[d],
                        device_id={"expert": peer},
                        device_id_type=MESH,
                    )
                )
    for copy in copies:
        copy.start()
    inward = (
        pltpu.make_async_copy(tok_ref.at[me], hold_tok, own_sem.at[0]),
        pltpu.make_async_copy(sig_ref.at[me], hold_sig, own_sem.at[1]),
        pltpu.make_async_copy(pay_ref, hold_pay, own_sem.at[2]),
    )
    for copy in inward:
        copy.start()
    for copy in inward:
        copy.wait()
    outward = (
        pltpu.make_async_copy(hold_tok, got_tok.at[me], own_sem.at[3]),
        pltpu.make_async_copy(hold_sig, got_sig.at[me], own_sem.at[4]),
        pltpu.make_async_copy(hold_pay, full.at[mine], own_sem.at[5]),
    )
    for copy in outward:
        copy.start()
    for copy in outward:
        copy.wait()
    for copy in copies:
        copy.wait()


def exchange(send_tokens, send_signal, payload, experts, groups):
    anywhere = pl.BlockSpec(memory_space=pl.ANY)
    dma = pltpu.SemaphoreType.DMA
    return pl.pallas_call(
        functools.partial(exchange_kernel, experts, groups),
        out_shape=(
            jax.ShapeDtypeStruct(send_tokens.shape, send_tokens.dtype),
            jax.ShapeDtypeStruct(send_signal.shape, send_signal.dtype),
            jax.ShapeDtypeStruct((groups,) + payload.shape, payload.dtype),
        ),
        in_specs=[anywhere] * 3,
        out_specs=(anywhere,) * 3,
        scratch_shapes=[
            pltpu.VMEM(send_tokens.shape[1:], send_tokens.dtype),
            pltpu.VMEM(send_signal.shape[1:], send_signal.dtype),
            pltpu.VMEM(payload.shape, payload.dtype),
            dma((experts,)), dma((experts,)), dma((experts,)), dma((experts,)),
            dma((groups,)), dma((groups,)), dma((6,)),
        ],
        compiler_params=pltpu.CompilerParams(collective_id=0, has_side_effects=True),
    )(send_tokens, send_signal, payload)


def chain_kernel(
    groups, part_ref, out_ref, from_left, from_right, to_right, to_left,
    right_send, right_recv, left_send, left_recv,
):
    mine = lax.axis_index("group")
    last = groups - 1
    side = part_ref.shape[1]
    barrier = pltpu.get_barrier_semaphore()

    for shift in (1, last):
        pl.semaphore_signal(
            barrier, inc=1, device_id={"group": lax.rem(mine + shift, groups)}, device_id_type=MESH
        )
    pl.semaphore_wait(barrier, 2)

    def rightward(k, src):
        return pltpu.make_async_remote_copy(
            src_ref=src.at[k],
            dst_ref=from_left.at[k],
            send_sem=right_send.at[k],
            recv_sem=right_recv.at[k],
            device_id={"group": lax.rem(mine + 1, groups)},
            device_id_type=MESH,
        )

    def leftward(k, src):
        return pltpu.make_async_remote_copy(
            src_ref=src.at[k],
            dst_ref=from_right.at[k],
            send_sem=left_send.at[k],
            recv_sem=left_recv.at[k],
            device_id={"group": lax.rem(mine + last, groups)},
            device_id_type=MESH,
        )

    pairs = [(r, c) for r in range(groups) for c in range(r, groups)]

    @pl.when(mine == 0)
    def _():
        for k in range(len(pairs)):
            rightward(k, part_ref).start()

    @pl.when(mine == last)
    def _():
        for k in range(len(pairs)):
            leftward(k, part_ref).start()

    def emit(k, total):
        r, c = pairs[k]
        out_ref[r * side : (r + 1) * side, c * side : (c + 1) * side] = total
        if c > r:
            out_ref[c * side : (c + 1) * side, r * side : (r + 1) * side] = total.T

    for k in range(len(pairs)):

        @pl.when(mine == 0)
        def _():
            leftward(k, to_left).wait_recv()
            emit(k, part_ref[k].astype(jnp.float32) + from_right[k].astype(jnp.float32))

        @pl.when(mine == last)
        def _():
            rightward(k, to_right).wait_recv()
            emit(k, part_ref[k].astype(jnp.float32) + from_left[k].astype(jnp.float32))

        @pl.when((mine > 0) & (mine < last))
        def _():
            own = part_ref[k].astype(jnp.float32)
            rightward(k, to_right).wait_recv()
            both = own + from_left[k].astype(jnp.float32)
            to_right[k] = both.astype(jnp.bfloat16)
            rightward(k, to_right).start()
            leftward(k, to_left).wait_recv()
            other = from_right[k].astype(jnp.float32)
            to_left[k] = (own + other).astype(jnp.bfloat16)
            leftward(k, to_left).start()
            emit(k, both + other)

    for k in range(len(pairs)):

        @pl.when(mine < last)
        def _():
            rightward(k, to_right).wait_send()

        @pl.when(mine > 0)
        def _():
            leftward(k, to_left).wait_send()


def chain_sum(part, groups):
    count, side = part.shape[0], part.shape[1]
    vmem = pl.BlockSpec(memory_space=pltpu.VMEM)
    dma = pltpu.SemaphoreType.DMA
    return pl.pallas_call(
        functools.partial(chain_kernel, groups),
        out_shape=jax.ShapeDtypeStruct((groups * side, groups * side), jnp.float32),
        in_specs=[vmem],
        out_specs=vmem,
        scratch_shapes=[pltpu.VMEM(part.shape, part.dtype)] * 4 + [dma((count,))] * 4,
        compiler_params=pltpu.CompilerParams(
            collective_id=1, has_side_effects=True, vmem_limit_bytes=32 << 20
        ),
    )(part)


def body(tokens, cotangent, routing, stat_prev, root_prev, owner_map):
    expert_count = lax.axis_size("expert")
    group_count = lax.axis_size("group")
    my_expert = lax.axis_index("expert")
    my_group = lax.axis_index("group")
    tok_rows = tokens.shape[0]
    width_part = tokens.shape[1]
    hidden = cotangent.shape[1]
    row_block = stat_prev.shape[1]
    capacity = 2 * tok_rows // expert_count
    owners = expert_count // 4
    route = routing[:, 0]
    order = jnp.arange(tok_rows, dtype=jnp.int32)
    earlier = (route[:, None] == route[None, :]) & (order[:, None] < order[None, :])
    position = jnp.sum(earlier.astype(jnp.int32), axis=0)
    column = route * capacity + position
    slots = jnp.arange(expert_count * capacity, dtype=jnp.int32)
    select = (slots[:, None] == column[None, :]).astype(jnp.bfloat16)
    send_tokens = jnp.dot(select, tokens, preferred_element_type=jnp.float32)
    send_tokens = send_tokens.astype(jnp.bfloat16).reshape(expert_count, capacity, width_part)
    send_signal = jnp.dot(select, cotangent, preferred_element_type=jnp.float32)
    send_signal = send_signal.astype(jnp.bfloat16).reshape(expert_count, capacity, hidden)
    my_live = jnp.take(owner_map, my_expert) < owners
    payload = jnp.where(my_live, stat_prev[0].astype(jnp.bfloat16), root_prev[0])
    got_tokens, got_signal, full = exchange(
        send_tokens, send_signal, payload, expert_count, group_count
    )
    got_tokens = got_tokens.reshape(expert_count * capacity, width_part)
    got_signal = got_signal.reshape(expert_count * capacity, hidden)
    full = full.reshape(hidden, hidden)
    grad = lax.dot_general(
        got_tokens, got_signal, (((0,), (0,)), ((), ())), preferred_element_type=jnp.float32
    )
    grad = (grad * (1.0 / math.sqrt(tok_rows))).astype(jnp.bfloat16)
    parts = []
    for r in range(group_count):
        panel = lax.dot_general(
            grad[:, r * row_block : (r + 1) * row_block],
            grad[:, r * row_block :],
            (((0,), (0,)), ((), ())),
            preferred_element_type=jnp.float32,
        ).astype(jnp.bfloat16)
        for c in range(group_count - r):
            parts.append(panel[:, c * row_block : (c + 1) * row_block])
    gram = chain_sum(jnp.stack(parts), group_count)
    share = (1.0 - keep_share) / (width_part * group_count)
    gram_rows = lax.dynamic_slice_in_dim(gram, my_group * row_block, row_block, 0)
    stat_new = keep_share * stat_prev[0] + share * gram_rows

    def refresh():
        return newton_root(
            (keep_share * full.astype(jnp.float32) + share * gram).astype(jnp.bfloat16)
        )

    root_full = lax.cond(my_live, refresh, lambda: full)
    update = jnp.dot(grad, root_full, preferred_element_type=jnp.float32).astype(jnp.bfloat16)
    root_rows = lax.dynamic_slice_in_dim(root_full, my_group * row_block, row_block, 0)
    return (stat_new[None], root_rows[None], update[None])


def solution(mesh):
    in_specs = (
        P("expert", "group"),
        P("expert", None),
        P("expert", None),
        P("expert", "group", None),
        P("expert", "group", None),
        P(),
    )
    out_specs = (P("expert", "group", None), P("expert", "group", None), P("expert", "group", None))
    return jax.shard_map(body, mesh=mesh, in_specs=in_specs, out_specs=out_specs, check_vma=False)
```

```python
import functools
import math

import jax
import jax.numpy as jnp
from jax import lax
from jax.experimental import pallas as pl
from jax.experimental.pallas import tpu as pltpu
from jax.sharding import PartitionSpec as P

ITERS = 2
POWER = 8
MESH = pl.DeviceIdType.MESH

keep_share = 0.9


def exchange_kernel(
    experts, groups, tok_ref, sig_ref, pay_ref, got_tok, got_sig, full,
    hold_tok, hold_sig, hold_pay, tok_send, tok_recv, sig_send, sig_recv, pay_send, pay_recv, own_sem,
):
    me = lax.axis_index("expert")
    mine = lax.axis_index("group")
    barrier = pltpu.get_barrier_semaphore()
    for d in range(1, experts):
        pl.semaphore_signal(
            barrier, inc=1, device_id={"expert": lax.rem(me + d, experts)}, device_id_type=MESH
        )
    for d in range(1, groups):
        pl.semaphore_signal(
            barrier, inc=1, device_id={"group": lax.rem(mine + d, groups)}, device_id_type=MESH
        )
    pl.semaphore_wait(barrier, experts + groups - 2)
    copies = []
    for d in range(1, max(experts, groups)):
        if d < groups:
            copies.append(
                pltpu.make_async_remote_copy(
                    src_ref=pay_ref,
                    dst_ref=full.at[mine],
                    send_sem=pay_send.at[d],
                    recv_sem=pay_recv.at[d],
                    device_id={"group": lax.rem(mine + d, groups)},
                    device_id_type=MESH,
                )
            )
        if d < experts:
            peer = lax.rem(me + d, experts)
            for src, dst, ssem, rsem in (
                (tok_ref, got_tok, tok_send, tok_recv),
                (sig_ref, got_sig, sig_send, sig_recv),
            ):
                copies.append(
                    pltpu.make_async_remote_copy(
                        src_ref=src.at[peer],
                        dst_ref=dst.at[me],
                        send_sem=ssem.at[d],
                        recv_sem=rsem.at[d],
                        device_id={"expert": peer},
                        device_id_type=MESH,
                    )
                )
    for copy in copies:
        copy.start()
    inward = (
        pltpu.make_async_copy(tok_ref.at[me], hold_tok, own_sem.at[0]),
        pltpu.make_async_copy(sig_ref.at[me], hold_sig, own_sem.at[1]),
        pltpu.make_async_copy(pay_ref, hold_pay, own_sem.at[2]),
    )
    for copy in inward:
        copy.start()
    for copy in inward:
        copy.wait()
    outward = (
        pltpu.make_async_copy(hold_tok, got_tok.at[me], own_sem.at[3]),
        pltpu.make_async_copy(hold_sig, got_sig.at[me], own_sem.at[4]),
        pltpu.make_async_copy(hold_pay, full.at[mine], own_sem.at[5]),
    )
    for copy in outward:
        copy.start()
    for copy in outward:
        copy.wait()
    for copy in copies:
        copy.wait()


def exchange(send_tokens, send_signal, payload, experts, groups):
    anywhere = pl.BlockSpec(memory_space=pl.ANY)
    dma = pltpu.SemaphoreType.DMA
    return pl.pallas_call(
        functools.partial(exchange_kernel, experts, groups),
        out_shape=(
            jax.ShapeDtypeStruct(send_tokens.shape, send_tokens.dtype),
            jax.ShapeDtypeStruct(send_signal.shape, send_signal.dtype),
            jax.ShapeDtypeStruct((groups,) + payload.shape, payload.dtype),
        ),
        in_specs=[anywhere] * 3,
        out_specs=(anywhere,) * 3,
        scratch_shapes=[
            pltpu.VMEM(send_tokens.shape[1:], send_tokens.dtype),
            pltpu.VMEM(send_signal.shape[1:], send_signal.dtype),
            pltpu.VMEM(payload.shape, payload.dtype),
            dma((experts,)), dma((experts,)), dma((experts,)), dma((experts,)),
            dma((groups,)), dma((groups,)), dma((6,)),
        ],
        compiler_params=pltpu.CompilerParams(collective_id=0, has_side_effects=True),
    )(send_tokens, send_signal, payload)


def chain_kernel(
    groups, share, part_ref, full_ref, prev_ref, low_ref, stat_ref,
    from_left, from_right, to_right, to_left, right_send, right_recv, left_send, left_recv,
):
    mine = lax.axis_index("group")
    last = groups - 1
    side = part_ref.shape[1]
    barrier = pltpu.get_barrier_semaphore()

    for shift in (1, last):
        pl.semaphore_signal(
            barrier, inc=1, device_id={"group": lax.rem(mine + shift, groups)}, device_id_type=MESH
        )
    pl.semaphore_wait(barrier, 2)

    def rightward(k, src):
        return pltpu.make_async_remote_copy(
            src_ref=src.at[k],
            dst_ref=from_left.at[k],
            send_sem=right_send.at[k],
            recv_sem=right_recv.at[k],
            device_id={"group": lax.rem(mine + 1, groups)},
            device_id_type=MESH,
        )

    def leftward(k, src):
        return pltpu.make_async_remote_copy(
            src_ref=src.at[k],
            dst_ref=from_right.at[k],
            send_sem=left_send.at[k],
            recv_sem=left_recv.at[k],
            device_id={"group": lax.rem(mine + last, groups)},
            device_id_type=MESH,
        )

    pairs = [(r, c) for r in range(groups) for c in range(r, groups)]

    @pl.when(mine == 0)
    def _():
        for k in range(len(pairs)):
            rightward(k, part_ref).start()

    @pl.when(mine == last)
    def _():
        for k in range(len(pairs)):
            leftward(k, part_ref).start()

    def emit(k, total):
        r, c = pairs[k]
        rows, columns = slice(r * side, (r + 1) * side), slice(c * side, (c + 1) * side)
        scaled = share * total
        low = keep_share * full_ref[r, :, columns].astype(jnp.float32) + scaled
        low_ref[rows, columns] = low.astype(jnp.bfloat16)

        @pl.when(mine == r)
        def _():
            stat_ref[:, columns] = keep_share * prev_ref[:, columns] + scaled

        if c > r:
            low_ref[columns, rows] = low.T.astype(jnp.bfloat16)

            @pl.when(mine == c)
            def _():
                stat_ref[:, rows] = keep_share * prev_ref[:, rows] + scaled.T

    def own(k):
        return part_ref[k].astype(jnp.float32)

    def pass_right(k):
        rightward(k, to_right).wait_recv()
        to_right[k] = (own(k) + from_left[k].astype(jnp.float32)).astype(jnp.bfloat16)
        rightward(k, to_right).start()

    def pass_left(k):
        leftward(k, to_left).wait_recv()
        to_left[k] = (own(k) + from_right[k].astype(jnp.float32)).astype(jnp.bfloat16)
        leftward(k, to_left).start()

    def finish(k):
        emit(k, own(k) + from_left[k].astype(jnp.float32) + from_right[k].astype(jnp.float32))

    count = len(pairs)

    @pl.when(mine == 0)
    def _():
        for k in range(count):
            leftward(k, to_left).wait_recv()
            emit(k, own(k) + from_right[k].astype(jnp.float32))

    @pl.when(mine == last)
    def _():
        for k in range(count):
            rightward(k, to_right).wait_recv()
            emit(k, own(k) + from_left[k].astype(jnp.float32))

    lag = 2
    for near, far, here in (
        (pass_right, pass_left, (mine > 0) & (2 * mine < last)),
        (pass_left, pass_right, (mine < last) & (2 * mine >= last)),
    ):

        @pl.when(here)
        def _():
            for step in range(count + lag):
                if step < count:
                    near(step)
                if step >= lag:
                    far(step - lag)
                    finish(step - lag)

    for k in range(count):

        @pl.when(mine < last)
        def _():
            rightward(k, to_right).wait_send()

        @pl.when(mine > 0)
        def _():
            leftward(k, to_left).wait_send()


def chain_sum(part, full, prev_rows, share, groups):
    count, side = part.shape[0], part.shape[1]
    vmem = pl.BlockSpec(memory_space=pltpu.VMEM)
    dma = pltpu.SemaphoreType.DMA
    return pl.pallas_call(
        functools.partial(chain_kernel, groups, share),
        out_shape=(
            jax.ShapeDtypeStruct((groups * side, groups * side), jnp.bfloat16),
            jax.ShapeDtypeStruct(prev_rows.shape, jnp.float32),
        ),
        in_specs=[vmem] * 3,
        out_specs=(vmem, vmem),
        scratch_shapes=[pltpu.VMEM(part.shape, part.dtype)] * 4 + [dma((count,))] * 4,
        compiler_params=pltpu.CompilerParams(
            collective_id=1, has_side_effects=True, vmem_limit_bytes=40 << 20
        ),
    )(part, full, prev_rows)


def root_kernel(
    groups, live_ref, low_ref, full_hbm, grad_hbm, rows_ref, update_hbm,
    grad_ref, factor, moment, square, fourth, root, result, sems,
):
    mine = lax.axis_index("group")
    order = low_ref.shape[0]
    side = order // groups
    fetch = pltpu.make_async_copy(grad_hbm, grad_ref, sems.at[0])
    fetch.start()
    live = live_ref[0] == 1

    @pl.when(live)
    def _():
        vector = jnp.full((16, order), 1.0 / math.sqrt(order), jnp.float32)
        length = jnp.ones((1, 1), jnp.float32)
        for turn_index in range(POWER):
            image = jnp.dot(
                vector.astype(jnp.bfloat16), low_ref[...], preferred_element_type=jnp.float32
            )
            first = image[:1]
            length = jnp.sqrt(jnp.sum(first * first, axis=1, keepdims=True))
            vector = image / length
        scaling = 2.5 / length
        outer = jnp.sqrt(jnp.sqrt(scaling))

        def tile(t):
            return pl.ds(pl.multiple_of(t * side, side), side)

        def factor_of(t, value):
            row = lax.broadcasted_iota(jnp.int32, (side, order), 0) + t * side
            column = lax.broadcasted_iota(jnp.int32, (side, order), 1)
            identity = (row == column).astype(jnp.float32)
            return ((5.0 * identity - value) * 0.25).astype(jnp.bfloat16)

        def product(left, right, t):
            return jnp.dot(left[tile(t), :], right[...], preferred_element_type=jnp.float32)

        @pl.loop(0, groups)
        def _(t):
            value = scaling * low_ref[tile(t), :].astype(jnp.float32)
            moment[tile(t), :] = value.astype(jnp.bfloat16)
            factor[tile(t), :] = factor_of(t, value)

        @pl.loop(0, groups)
        def _(t):
            square[tile(t), :] = product(factor, factor, t).astype(jnp.bfloat16)

        @pl.loop(0, groups)
        def _(t):
            fourth[tile(t), :] = product(square, square, t).astype(jnp.bfloat16)

        @pl.loop(0, groups)
        def _(t):
            root[tile(t), :] = factor_of(t, product(fourth, moment, t))

        @pl.loop(0, groups)
        def _(t):
            square[tile(t), :] = (outer * product(factor, root, t)).astype(jnp.bfloat16)

    @pl.when(jnp.logical_not(live))
    def _():
        prior = pltpu.make_async_copy(full_hbm, square, sems.at[1])
        prior.start()
        prior.wait()

    rows_ref[...] = square[pl.ds(pl.multiple_of(mine * side, side), side), :]
    fetch.wait()
    tall = grad_ref.shape[0] // groups
    sends = []
    for t in range(groups):
        part = slice(t * tall, (t + 1) * tall)
        result[part, :] = jnp.dot(
            grad_ref[part, :], square[...], preferred_element_type=jnp.float32
        ).astype(jnp.bfloat16)
        sends.append(
            pltpu.make_async_copy(result.at[part, :], update_hbm.at[part, :], sems.at[2 + t])
        )
        sends[-1].start()
    for send in sends:
        send.wait()


def finish_roots(live, low, full, grad, groups):
    order = low.shape[0]
    vmem = pl.BlockSpec(memory_space=pltpu.VMEM)
    anywhere = pl.BlockSpec(memory_space=pl.ANY)
    square = pltpu.VMEM((order, order), jnp.bfloat16)
    tall = pltpu.VMEM(grad.shape, jnp.bfloat16)
    return pl.pallas_call(
        functools.partial(root_kernel, groups),
        out_shape=(
            jax.ShapeDtypeStruct((order // groups, order), jnp.bfloat16),
            jax.ShapeDtypeStruct(grad.shape, jnp.bfloat16),
        ),
        in_specs=[pl.BlockSpec(memory_space=pltpu.SMEM), vmem, anywhere, anywhere],
        out_specs=(vmem, anywhere),
        scratch_shapes=[
            tall, square, square, square, square, square, tall,
            pltpu.SemaphoreType.DMA((2 + groups,)),
        ],
        compiler_params=pltpu.CompilerParams(vmem_limit_bytes=40 << 20),
    )(live, low, full, grad)


def body(tokens, cotangent, routing, stat_prev, root_prev, owner_map):
    expert_count = lax.axis_size("expert")
    group_count = lax.axis_size("group")
    my_expert = lax.axis_index("expert")
    my_group = lax.axis_index("group")
    tok_rows = tokens.shape[0]
    width_part = tokens.shape[1]
    hidden = cotangent.shape[1]
    row_block = stat_prev.shape[1]
    capacity = 2 * tok_rows // expert_count
    owners = expert_count // 4
    route = routing[:, 0]
    order = jnp.arange(tok_rows, dtype=jnp.int32)
    earlier = (route[:, None] == route[None, :]) & (order[:, None] < order[None, :])
    position = jnp.sum(earlier.astype(jnp.int32), axis=0)
    column = route * capacity + position
    slots = jnp.arange(expert_count * capacity, dtype=jnp.int32)
    select = (slots[:, None] == column[None, :]).astype(jnp.bfloat16)
    send_tokens = jnp.dot(select, tokens, preferred_element_type=jnp.float32)
    send_tokens = send_tokens.astype(jnp.bfloat16).reshape(expert_count, capacity, width_part)
    send_signal = jnp.dot(select, cotangent, preferred_element_type=jnp.float32)
    send_signal = send_signal.astype(jnp.bfloat16).reshape(expert_count, capacity, hidden)
    my_live = jnp.take(owner_map, my_expert) < owners
    payload = jnp.where(my_live, stat_prev[0].astype(jnp.bfloat16), root_prev[0])
    got_tokens, got_signal, full = exchange(
        send_tokens, send_signal, payload, expert_count, group_count
    )
    got_tokens = got_tokens.reshape(expert_count * capacity, width_part)
    got_signal = got_signal.reshape(expert_count * capacity, hidden)
    grad = lax.dot_general(
        got_tokens, got_signal, (((0,), (0,)), ((), ())), preferred_element_type=jnp.float32
    )
    grad = (grad * (1.0 / math.sqrt(tok_rows))).astype(jnp.bfloat16)
    parts = []
    for r in range(group_count):
        panel = lax.dot_general(
            grad[:, r * row_block : (r + 1) * row_block],
            grad[:, r * row_block :],
            (((0,), (0,)), ((), ())),
            preferred_element_type=jnp.float32,
        ).astype(jnp.bfloat16)
        for c in range(group_count - r):
            parts.append(panel[:, c * row_block : (c + 1) * row_block])
    share = (1.0 - keep_share) / (width_part * group_count)
    stat_low, stat_new = chain_sum(jnp.stack(parts), full, stat_prev[0], share, group_count)
    live_flag = my_live.astype(jnp.int32).reshape(1)
    root_rows, update = finish_roots(
        live_flag, stat_low, full.reshape(hidden, hidden), grad, group_count
    )
    return (stat_new[None], root_rows[None], update[None])


def solution(mesh):
    in_specs = (
        P("expert", "group"),
        P("expert", None),
        P("expert", None),
        P("expert", "group", None),
        P("expert", "group", None),
        P(),
    )
    out_specs = (P("expert", "group", None), P("expert", "group", None), P("expert", "group", None))
    return jax.shard_map(body, mesh=mesh, in_specs=in_specs, out_specs=out_specs, check_vma=False)
```

```python
import functools
import math

import jax
import jax.numpy as jnp
from jax import lax
from jax.experimental import pallas as pl
from jax.experimental.pallas import tpu as pltpu
from jax.sharding import PartitionSpec as P

ITERS = 2
POWER = 8
MESH = pl.DeviceIdType.MESH

keep_share = 0.9


def prepare_kernel(
    capacity, owners, pieces, owner_ref, tall_ref, wide_ref, tok_ref, sig_ref, prev_ref, old_ref,
    tok_hbm, sig_hbm, pay_hbm, tok_out, sig_out, pay_out, sems,
):
    tok_rows = tok_ref.shape[0]
    live = owner_ref[lax.axis_index("expert")] < owners
    pay_out[...] = jnp.where(live, prev_ref[...].astype(jnp.bfloat16), old_ref[...])
    sends = [pltpu.make_async_copy(pay_out, pay_hbm, sems.at[2 * pieces])]
    sends[0].start()
    wide = wide_ref[...]
    before = lax.broadcasted_iota(jnp.int32, (tok_rows, tok_rows), 0)
    after = lax.broadcasted_iota(jnp.int32, (tok_rows, tok_rows), 1)
    earlier = jnp.where((tall_ref[...] == wide) & (before < after), 1, 0)
    column = wide * capacity + jnp.sum(earlier, axis=0, keepdims=True)
    piece = tok_out.shape[0] // pieces
    for t in range(pieces):
        rows = slice(t * piece, (t + 1) * piece)
        slots = lax.broadcasted_iota(jnp.int32, (piece, tok_rows), 0) + t * piece
        select = (slots == column).astype(jnp.float32).astype(jnp.bfloat16)
        for which, (src, out, hbm) in enumerate(
            ((tok_ref, tok_out, tok_hbm), (sig_ref, sig_out, sig_hbm))
        ):
            out[rows, :] = jnp.dot(
                select, src[...], preferred_element_type=jnp.float32
            ).astype(jnp.bfloat16)
            sends.append(
                pltpu.make_async_copy(
                    out.at[rows, :], hbm.at[rows, :], sems.at[2 * t + which]
                )
            )
            sends[-1].start()
    for send in sends:
        send.wait()


def prepare(owner_map, routing, tokens, cotangent, prev_rows, old_rows, experts, capacity, owners):
    slots = experts * capacity
    pieces = 4 if slots % 64 == 0 else 1
    vmem = pl.BlockSpec(memory_space=pltpu.VMEM)
    anywhere = pl.BlockSpec(memory_space=pl.ANY)
    shapes = (
        (slots, tokens.shape[1]), (slots, cotangent.shape[1]), prev_rows.shape,
    )
    return pl.pallas_call(
        functools.partial(prepare_kernel, capacity, owners, pieces),
        out_shape=tuple(jax.ShapeDtypeStruct(shape, jnp.bfloat16) for shape in shapes),
        in_specs=[pl.BlockSpec(memory_space=pltpu.SMEM)] + [vmem] * 6,
        out_specs=(anywhere,) * 3,
        scratch_shapes=[pltpu.VMEM(shape, jnp.bfloat16) for shape in shapes]
        + [pltpu.SemaphoreType.DMA((2 * pieces + 1,))],
        compiler_params=pltpu.CompilerParams(vmem_limit_bytes=40 << 20),
    )(owner_map, routing, routing.reshape(1, -1), tokens, cotangent, prev_rows, old_rows)


def exchange_kernel(
    experts, groups, tok_ref, sig_ref, pay_ref, got_tok, got_sig, full,
    hold_tok, hold_sig, hold_pay, tok_send, tok_recv, sig_send, sig_recv, pay_send, pay_recv, own_sem,
):
    me = lax.axis_index("expert")
    mine = lax.axis_index("group")
    barrier = pltpu.get_barrier_semaphore()
    for d in range(1, experts):
        pl.semaphore_signal(
            barrier, inc=1, device_id={"expert": lax.rem(me + d, experts)}, device_id_type=MESH
        )
    for d in (1, groups - 1):
        pl.semaphore_signal(
            barrier, inc=1, device_id={"group": lax.rem(mine + d, groups)}, device_id_type=MESH
        )
    pl.semaphore_wait(barrier, experts + 1)
    last = groups - 1

    def relay(d, step, src):
        origin = lax.rem(mine + (groups - d) * step, groups)
        return pltpu.make_async_remote_copy(
            src_ref=full.at[origin] if src is None else src,
            dst_ref=full.at[origin],
            send_sem=pay_send.at[0 if d == 1 else 1, step],
            recv_sem=pay_recv.at[0 if d == 1 else 1, step],
            device_id={"group": lax.rem(mine + d, groups)},
            device_id_type=MESH,
        )

    @pl.when(mine < last)
    def _():
        relay(1, 0, pay_ref).start()

    @pl.when(mine > 0)
    def _():
        relay(last, 0, pay_ref).start()

    copies = []
    for d in range(1, experts):
        peer = lax.rem(me + d, experts)
        for src, dst, ssem, rsem in (
            (tok_ref, got_tok, tok_send, tok_recv),
            (sig_ref, got_sig, sig_send, sig_recv),
        ):
            copies.append(
                pltpu.make_async_remote_copy(
                    src_ref=src.at[peer],
                    dst_ref=dst.at[me],
                    send_sem=ssem.at[d],
                    recv_sem=rsem.at[d],
                    device_id={"expert": peer},
                    device_id_type=MESH,
                )
            )
    for copy in copies:
        copy.start()
    inward = (
        pltpu.make_async_copy(tok_ref.at[me], hold_tok, own_sem.at[0]),
        pltpu.make_async_copy(sig_ref.at[me], hold_sig, own_sem.at[1]),
        pltpu.make_async_copy(pay_ref, hold_pay, own_sem.at[2]),
    )
    for copy in inward:
        copy.start()
    for copy in inward:
        copy.wait()
    outward = (
        pltpu.make_async_copy(hold_tok, got_tok.at[me], own_sem.at[3]),
        pltpu.make_async_copy(hold_sig, got_sig.at[me], own_sem.at[4]),
        pltpu.make_async_copy(hold_pay, full.at[mine], own_sem.at[5]),
    )
    for copy in outward:
        copy.start()
    for copy in outward:
        copy.wait()
    for step in range(last):

        @pl.when(mine > step)
        def _():
            relay(1, step, None).wait_recv()

        @pl.when((mine > step) & (mine < last))
        def _():
            relay(1, step + 1, None).start()

        @pl.when(last - mine > step)
        def _():
            relay(last, step, None).wait_recv()

        @pl.when((last - mine > step) & (mine > 0))
        def _():
            relay(last, step + 1, None).start()

    for step in range(groups):

        @pl.when((mine >= step) & (mine < last))
        def _():
            relay(1, step, None).wait_send()

        @pl.when((last - mine >= step) & (mine > 0))
        def _():
            relay(last, step, None).wait_send()

    for copy in copies:
        copy.wait()


def exchange(send_tokens, send_signal, payload, experts, groups):
    anywhere = pl.BlockSpec(memory_space=pl.ANY)
    dma = pltpu.SemaphoreType.DMA
    return pl.pallas_call(
        functools.partial(exchange_kernel, experts, groups),
        out_shape=(
            jax.ShapeDtypeStruct(send_tokens.shape, send_tokens.dtype),
            jax.ShapeDtypeStruct(send_signal.shape, send_signal.dtype),
            jax.ShapeDtypeStruct((groups,) + payload.shape, payload.dtype),
        ),
        in_specs=[anywhere] * 3,
        out_specs=(anywhere,) * 3,
        scratch_shapes=[
            pltpu.VMEM(send_tokens.shape[1:], send_tokens.dtype),
            pltpu.VMEM(send_signal.shape[1:], send_signal.dtype),
            pltpu.VMEM(payload.shape, payload.dtype),
            dma((experts,)), dma((experts,)), dma((experts,)), dma((experts,)),
            dma((2, groups)), dma((2, groups)), dma((6,)),
        ],
        compiler_params=pltpu.CompilerParams(collective_id=0, has_side_effects=True),
    )(send_tokens, send_signal, payload)


def chain_kernel(
    groups, share, part_ref, full_ref, prev_ref, low_ref, stat_ref,
    from_left, from_right, to_right, to_left, right_send, right_recv, left_send, left_recv,
):
    mine = lax.axis_index("group")
    last = groups - 1
    side = part_ref.shape[1]
    barrier = pltpu.get_barrier_semaphore()

    for shift in (1, last):
        pl.semaphore_signal(
            barrier, inc=1, device_id={"group": lax.rem(mine + shift, groups)}, device_id_type=MESH
        )
    pl.semaphore_wait(barrier, 2)

    def rightward(k, src):
        return pltpu.make_async_remote_copy(
            src_ref=src.at[k],
            dst_ref=from_left.at[k],
            send_sem=right_send.at[k],
            recv_sem=right_recv.at[k],
            device_id={"group": lax.rem(mine + 1, groups)},
            device_id_type=MESH,
        )

    def leftward(k, src):
        return pltpu.make_async_remote_copy(
            src_ref=src.at[k],
            dst_ref=from_right.at[k],
            send_sem=left_send.at[k],
            recv_sem=left_recv.at[k],
            device_id={"group": lax.rem(mine + last, groups)},
            device_id_type=MESH,
        )

    pairs = [(r, c) for r in range(groups) for c in range(r, groups)]

    @pl.when(mine == 0)
    def _():
        for k in range(len(pairs)):
            rightward(k, part_ref).start()

    @pl.when(mine == last)
    def _():
        for k in range(len(pairs)):
            leftward(k, part_ref).start()

    def emit(k, total):
        r, c = pairs[k]
        rows, columns = slice(r * side, (r + 1) * side), slice(c * side, (c + 1) * side)
        scaled = share * total
        low = keep_share * full_ref[r, :, columns].astype(jnp.float32) + scaled
        low_ref[rows, columns] = low.astype(jnp.bfloat16)

        @pl.when(mine == r)
        def _():
            stat_ref[:, columns] = keep_share * prev_ref[:, columns] + scaled

        if c > r:
            low_ref[columns, rows] = low.T.astype(jnp.bfloat16)

            @pl.when(mine == c)
            def _():
                stat_ref[:, rows] = keep_share * prev_ref[:, rows] + scaled.T

    def own(k):
        return part_ref[k].astype(jnp.float32)

    def pass_right(k):
        rightward(k, to_right).wait_recv()
        to_right[k] = (own(k) + from_left[k].astype(jnp.float32)).astype(jnp.bfloat16)
        rightward(k, to_right).start()

    def pass_left(k):
        leftward(k, to_left).wait_recv()
        to_left[k] = (own(k) + from_right[k].astype(jnp.float32)).astype(jnp.bfloat16)
        leftward(k, to_left).start()

    def finish(k):
        emit(k, own(k) + from_left[k].astype(jnp.float32) + from_right[k].astype(jnp.float32))

    count = len(pairs)

    @pl.when(mine == 0)
    def _():
        for k in range(count):
            leftward(k, to_left).wait_recv()
            emit(k, own(k) + from_right[k].astype(jnp.float32))

    @pl.when(mine == last)
    def _():
        for k in range(count):
            rightward(k, to_right).wait_recv()
            emit(k, own(k) + from_left[k].astype(jnp.float32))

    lag = 2
    for near, far, here in (
        (pass_right, pass_left, (mine > 0) & (2 * mine < last)),
        (pass_left, pass_right, (mine < last) & (2 * mine >= last)),
    ):

        @pl.when(here)
        def _():
            for step in range(count + lag):
                if step < count:
                    near(step)
                if step >= lag:
                    far(step - lag)
                    finish(step - lag)

    for k in range(count):

        @pl.when(mine < last)
        def _():
            rightward(k, to_right).wait_send()

        @pl.when(mine > 0)
        def _():
            leftward(k, to_left).wait_send()


def chain_sum(part, full, prev_rows, share, groups):
    count, side = part.shape[0], part.shape[1]
    vmem = pl.BlockSpec(memory_space=pltpu.VMEM)
    dma = pltpu.SemaphoreType.DMA
    return pl.pallas_call(
        functools.partial(chain_kernel, groups, share),
        out_shape=(
            jax.ShapeDtypeStruct((groups * side, groups * side), jnp.bfloat16),
            jax.ShapeDtypeStruct(prev_rows.shape, jnp.float32),
        ),
        in_specs=[vmem] * 3,
        out_specs=(vmem, vmem),
        scratch_shapes=[pltpu.VMEM(part.shape, part.dtype)] * 4 + [dma((count,))] * 4,
        compiler_params=pltpu.CompilerParams(
            collective_id=1, has_side_effects=True, vmem_limit_bytes=40 << 20
        ),
    )(part, full, prev_rows)


def root_kernel(
    groups, owners, owner_ref, low_ref, full_hbm, grad_hbm, stat_hbm, rows_ref, update_hbm, new_hbm,
    stat_ref, grad_ref, factor, moment, square, fourth, root, result, sems,
):
    mine = lax.axis_index("group")
    order = low_ref.shape[0]
    side = order // groups
    fetch = pltpu.make_async_copy(grad_hbm, grad_ref, sems.at[0])
    fetch.start()
    take = pltpu.make_async_copy(stat_hbm, stat_ref, sems.at[2 + groups])
    take.start()
    live = owner_ref[lax.axis_index("expert")] < owners
    take.wait()
    give = pltpu.make_async_copy(stat_ref, new_hbm, sems.at[3 + groups])
    give.start()

    @pl.when(live)
    def _():
        vector = jnp.full((16, order), 1.0 / math.sqrt(order), jnp.float32)
        length = jnp.ones((1, 1), jnp.float32)
        for turn_index in range(POWER):
            image = jnp.dot(
                vector.astype(jnp.bfloat16), low_ref[...], preferred_element_type=jnp.float32
            )
            first = image[:1]
            length = jnp.sqrt(jnp.sum(first * first, axis=1, keepdims=True))
            vector = image / length
        scaling = 2.5 / length
        outer = jnp.sqrt(jnp.sqrt(scaling))

        def tile(t):
            return pl.ds(pl.multiple_of(t * side, side), side)

        def factor_of(t, value):
            row = lax.broadcasted_iota(jnp.int32, (side, order), 0) + t * side
            column = lax.broadcasted_iota(jnp.int32, (side, order), 1)
            identity = (row == column).astype(jnp.float32)
            return ((5.0 * identity - value) * 0.25).astype(jnp.bfloat16)

        def product(left, right, t):
            return jnp.dot(left[tile(t), :], right[...], preferred_element_type=jnp.float32)

        @pl.loop(0, groups)
        def _(t):
            value = scaling * low_ref[tile(t), :].astype(jnp.float32)
            moment[tile(t), :] = value.astype(jnp.bfloat16)
            factor[tile(t), :] = factor_of(t, value)

        @pl.loop(0, groups)
        def _(t):
            square[tile(t), :] = product(factor, factor, t).astype(jnp.bfloat16)

        @pl.loop(0, groups)
        def _(t):
            fourth[tile(t), :] = product(square, square, t).astype(jnp.bfloat16)

        @pl.loop(0, groups)
        def _(t):
            root[tile(t), :] = factor_of(t, product(fourth, moment, t))

        @pl.loop(0, groups)
        def _(t):
            square[tile(t), :] = (outer * product(factor, root, t)).astype(jnp.bfloat16)

    @pl.when(jnp.logical_not(live))
    def _():
        prior = pltpu.make_async_copy(full_hbm, square, sems.at[1])
        prior.start()
        prior.wait()

    rows_ref[...] = square[pl.ds(pl.multiple_of(mine * side, side), side), :]
    fetch.wait()
    tall = grad_ref.shape[0] // groups
    sends = []
    for t in range(groups):
        part = slice(t * tall, (t + 1) * tall)
        result[part, :] = jnp.dot(
            grad_ref[part, :], square[...], preferred_element_type=jnp.float32
        ).astype(jnp.bfloat16)
        sends.append(
            pltpu.make_async_copy(result.at[part, :], update_hbm.at[part, :], sems.at[2 + t])
        )
        sends[-1].start()
    for send in sends:
        send.wait()
    give.wait()


def finish_roots(owner_map, low, full, grad, stat, groups, owners):
    order = low.shape[0]
    vmem = pl.BlockSpec(memory_space=pltpu.VMEM)
    anywhere = pl.BlockSpec(memory_space=pl.ANY)
    square = pltpu.VMEM((order, order), jnp.bfloat16)
    tall = pltpu.VMEM(grad.shape, jnp.bfloat16)
    return pl.pallas_call(
        functools.partial(root_kernel, groups, owners),
        out_shape=(
            jax.ShapeDtypeStruct((order // groups, order), jnp.bfloat16),
            jax.ShapeDtypeStruct(grad.shape, jnp.bfloat16),
            jax.ShapeDtypeStruct(stat.shape, jnp.float32),
        ),
        in_specs=[pl.BlockSpec(memory_space=pltpu.SMEM), vmem] + [anywhere] * 3,
        out_specs=(vmem, anywhere, anywhere),
        scratch_shapes=[
            pltpu.VMEM(stat.shape, jnp.float32), tall, square, square, square, square, square, tall,
            pltpu.SemaphoreType.DMA((4 + groups,)),
        ],
        compiler_params=pltpu.CompilerParams(vmem_limit_bytes=40 << 20),
    )(owner_map, low, full, grad, stat)


def body(tokens, cotangent, routing, stat_prev, root_prev, owner_map):
    expert_count = lax.axis_size("expert")
    group_count = lax.axis_size("group")
    tok_rows = tokens.shape[0]
    width_part = tokens.shape[1]
    hidden = cotangent.shape[1]
    row_block = stat_prev.shape[1]
    capacity = 2 * tok_rows // expert_count
    owners = expert_count // 4
    send_tokens, send_signal, payload = prepare(
        owner_map, routing, tokens, cotangent, stat_prev[0], root_prev[0],
        expert_count, capacity, owners,
    )
    send_tokens = send_tokens.reshape(expert_count, capacity, width_part)
    send_signal = send_signal.reshape(expert_count, capacity, hidden)
    got_tokens, got_signal, full = exchange(
        send_tokens, send_signal, payload, expert_count, group_count
    )
    got_tokens = got_tokens.reshape(expert_count * capacity, width_part)
    got_signal = got_signal.reshape(expert_count * capacity, hidden)
    grad = lax.dot_general(
        got_tokens, got_signal, (((0,), (0,)), ((), ())), preferred_element_type=jnp.float32
    )
    grad = (grad * (1.0 / math.sqrt(tok_rows))).astype(jnp.bfloat16)
    parts = []
    for r in range(group_count):
        panel = lax.dot_general(
            grad[:, r * row_block : (r + 1) * row_block],
            grad[:, r * row_block :],
            (((0,), (0,)), ((), ())),
            preferred_element_type=jnp.float32,
        ).astype(jnp.bfloat16)
        for c in range(group_count - r):
            parts.append(panel[:, c * row_block : (c + 1) * row_block])
    share = (1.0 - keep_share) / (width_part * group_count)
    stat_low, stat_new = chain_sum(jnp.stack(parts), full, stat_prev[0], share, group_count)
    root_rows, update, stat_new = finish_roots(
        owner_map, stat_low, full.reshape(hidden, hidden), grad, stat_new, group_count, owners
    )
    return (stat_new[None], root_rows[None], update[None])


def solution(mesh):
    in_specs = (
        P("expert", "group"),
        P("expert", None),
        P("expert", None),
        P("expert", "group", None),
        P("expert", "group", None),
        P(),
    )
    out_specs = (P("expert", "group", None), P("expert", "group", None), P("expert", "group", None))
    return jax.shard_map(body, mesh=mesh, in_specs=in_specs, out_specs=out_specs, check_vma=False)
```

```python
import functools
import math

import jax
import jax.numpy as jnp
from jax import lax
from jax.experimental import pallas as pl
from jax.experimental.pallas import tpu as pltpu
from jax.sharding import PartitionSpec as P

ITERS = 2
POWER = 8
MESH = pl.DeviceIdType.MESH

keep_share = 0.9


def prepare_kernel(
    capacity, owners, pieces, owner_ref, tall_ref, wide_ref, tok_ref, sig_ref, prev_ref, old_ref,
    tok_hbm, sig_hbm, pay_hbm, tok_out, sig_out, pay_out, sems,
):
    tok_rows = tok_ref.shape[0]
    live = owner_ref[lax.axis_index("expert")] < owners
    pay_out[...] = jnp.where(live, prev_ref[...].astype(jnp.bfloat16), old_ref[...])
    sends = [pltpu.make_async_copy(pay_out, pay_hbm, sems.at[2 * pieces])]
    sends[0].start()
    wide = wide_ref[...]
    before = lax.broadcasted_iota(jnp.int32, (tok_rows, tok_rows), 0)
    after = lax.broadcasted_iota(jnp.int32, (tok_rows, tok_rows), 1)
    earlier = jnp.where((tall_ref[...] == wide) & (before < after), 1, 0)
    column = wide * capacity + jnp.sum(earlier, axis=0, keepdims=True)
    piece = tok_out.shape[0] // pieces
    for t in range(pieces):
        rows = slice(t * piece, (t + 1) * piece)
        slots = lax.broadcasted_iota(jnp.int32, (piece, tok_rows), 0) + t * piece
        select = (slots == column).astype(jnp.float32).astype(jnp.bfloat16)
        for which, (src, out, hbm) in enumerate(
            ((tok_ref, tok_out, tok_hbm), (sig_ref, sig_out, sig_hbm))
        ):
            out[rows, :] = jnp.dot(
                select, src[...], preferred_element_type=jnp.float32
            ).astype(jnp.bfloat16)
            sends.append(
                pltpu.make_async_copy(
                    out.at[rows, :], hbm.at[rows, :], sems.at[2 * t + which]
                )
            )
            sends[-1].start()
    for send in sends:
        send.wait()


def prepare(owner_map, routing, tokens, cotangent, prev_rows, old_rows, experts, capacity, owners):
    slots = experts * capacity
    pieces = 4 if slots % 64 == 0 else 1
    vmem = pl.BlockSpec(memory_space=pltpu.VMEM)
    anywhere = pl.BlockSpec(memory_space=pl.ANY)
    shapes = (
        (slots, tokens.shape[1]), (slots, cotangent.shape[1]), prev_rows.shape,
    )
    return pl.pallas_call(
        functools.partial(prepare_kernel, capacity, owners, pieces),
        out_shape=tuple(jax.ShapeDtypeStruct(shape, jnp.bfloat16) for shape in shapes),
        in_specs=[pl.BlockSpec(memory_space=pltpu.SMEM)] + [vmem] * 6,
        out_specs=(anywhere,) * 3,
        scratch_shapes=[pltpu.VMEM(shape, jnp.bfloat16) for shape in shapes]
        + [pltpu.SemaphoreType.DMA((2 * pieces + 1,))],
    )(owner_map, routing, routing.reshape(1, -1), tokens, cotangent, prev_rows, old_rows)


def exchange_kernel(
    experts, groups, tok_ref, sig_ref, pay_ref, got_tok, got_sig, full,
    hold_tok, hold_sig, hold_pay, tok_send, tok_recv, sig_send, sig_recv, pay_send, pay_recv, own_sem,
):
    me = lax.axis_index("expert")
    mine = lax.axis_index("group")
    barrier = pltpu.get_barrier_semaphore()
    for d in range(1, experts):
        pl.semaphore_signal(
            barrier, inc=1, device_id={"expert": lax.rem(me + d, experts)}, device_id_type=MESH
        )
    for d in (1, groups - 1):
        pl.semaphore_signal(
            barrier, inc=1, device_id={"group": lax.rem(mine + d, groups)}, device_id_type=MESH
        )
    pl.semaphore_wait(barrier, experts + 1)
    last = groups - 1

    def relay(d, step, src):
        origin = lax.rem(mine + (groups - d) * step, groups)
        return pltpu.make_async_remote_copy(
            src_ref=full.at[origin] if src is None else src,
            dst_ref=full.at[origin],
            send_sem=pay_send.at[0 if d == 1 else 1, step],
            recv_sem=pay_recv.at[0 if d == 1 else 1, step],
            device_id={"group": lax.rem(mine + d, groups)},
            device_id_type=MESH,
        )

    @pl.when(mine < last)
    def _():
        relay(1, 0, pay_ref).start()

    @pl.when(mine > 0)
    def _():
        relay(last, 0, pay_ref).start()

    copies = []
    for d in range(1, experts):
        peer = lax.rem(me + d, experts)
        for src, dst, ssem, rsem in (
            (tok_ref, got_tok, tok_send, tok_recv),
            (sig_ref, got_sig, sig_send, sig_recv),
        ):
            copies.append(
                pltpu.make_async_remote_copy(
                    src_ref=src.at[peer],
                    dst_ref=dst.at[me],
                    send_sem=ssem.at[d],
                    recv_sem=rsem.at[d],
                    device_id={"expert": peer},
                    device_id_type=MESH,
                )
            )
    for copy in copies:
        copy.start()
    inward = (
        pltpu.make_async_copy(tok_ref.at[me], hold_tok, own_sem.at[0]),
        pltpu.make_async_copy(sig_ref.at[me], hold_sig, own_sem.at[1]),
        pltpu.make_async_copy(pay_ref, hold_pay, own_sem.at[2]),
    )
    for copy in inward:
        copy.start()
    for copy in inward:
        copy.wait()
    outward = (
        pltpu.make_async_copy(hold_tok, got_tok.at[me], own_sem.at[3]),
        pltpu.make_async_copy(hold_sig, got_sig.at[me], own_sem.at[4]),
        pltpu.make_async_copy(hold_pay, full.at[mine], own_sem.at[5]),
    )
    for copy in outward:
        copy.start()
    for copy in outward:
        copy.wait()
    for step in range(last):

        @pl.when(mine > step)
        def _():
            relay(1, step, None).wait_recv()

        @pl.when((mine > step) & (mine < last))
        def _():
            relay(1, step + 1, None).start()

        @pl.when(last - mine > step)
        def _():
            relay(last, step, None).wait_recv()

        @pl.when((last - mine > step) & (mine > 0))
        def _():
            relay(last, step + 1, None).start()

    for step in range(groups):

        @pl.when((mine >= step) & (mine < last))
        def _():
            relay(1, step, None).wait_send()

        @pl.when((last - mine >= step) & (mine > 0))
        def _():
            relay(last, step, None).wait_send()

    for copy in copies:
        copy.wait()


def exchange(send_tokens, send_signal, payload, experts, groups):
    anywhere = pl.BlockSpec(memory_space=pl.ANY)
    dma = pltpu.SemaphoreType.DMA
    return pl.pallas_call(
        functools.partial(exchange_kernel, experts, groups),
        out_shape=(
            jax.ShapeDtypeStruct(send_tokens.shape, send_tokens.dtype),
            jax.ShapeDtypeStruct(send_signal.shape, send_signal.dtype),
            jax.ShapeDtypeStruct((groups,) + payload.shape, payload.dtype),
        ),
        in_specs=[anywhere] * 3,
        out_specs=(anywhere,) * 3,
        scratch_shapes=[
            pltpu.VMEM(send_tokens.shape[1:], send_tokens.dtype),
            pltpu.VMEM(send_signal.shape[1:], send_signal.dtype),
            pltpu.VMEM(payload.shape, payload.dtype),
            dma((experts,)), dma((experts,)), dma((experts,)), dma((experts,)),
            dma((2, groups)), dma((2, groups)), dma((6,)),
        ],
        compiler_params=pltpu.CompilerParams(collective_id=0, has_side_effects=True),
    )(send_tokens, send_signal, payload)


def chain_kernel(
    groups, share, part_ref, full_ref, prev_ref, low_ref, stat_ref,
    from_left, from_right, to_right, to_left, right_send, right_recv, left_send, left_recv,
):
    mine = lax.axis_index("group")
    last = groups - 1
    side = part_ref.shape[1]
    barrier = pltpu.get_barrier_semaphore()

    for shift in (1, last):
        pl.semaphore_signal(
            barrier, inc=1, device_id={"group": lax.rem(mine + shift, groups)}, device_id_type=MESH
        )
    pl.semaphore_wait(barrier, 2)

    def rightward(k, src):
        return pltpu.make_async_remote_copy(
            src_ref=src.at[k],
            dst_ref=from_left.at[k],
            send_sem=right_send.at[k],
            recv_sem=right_recv.at[k],
            device_id={"group": lax.rem(mine + 1, groups)},
            device_id_type=MESH,
        )

    def leftward(k, src):
        return pltpu.make_async_remote_copy(
            src_ref=src.at[k],
            dst_ref=from_right.at[k],
            send_sem=left_send.at[k],
            recv_sem=left_recv.at[k],
            device_id={"group": lax.rem(mine + last, groups)},
            device_id_type=MESH,
        )

    pairs = [(r, c) for r in range(groups) for c in range(r, groups)]

    @pl.when(mine == 0)
    def _():
        for k in range(len(pairs)):
            rightward(k, part_ref).start()

    @pl.when(mine == last)
    def _():
        for k in range(len(pairs)):
            leftward(k, part_ref).start()

    def emit(k, total):
        r, c = pairs[k]
        rows, columns = slice(r * side, (r + 1) * side), slice(c * side, (c + 1) * side)
        scaled = share * total
        low = keep_share * full_ref[r, :, columns].astype(jnp.float32) + scaled
        low_ref[rows, columns] = low.astype(jnp.bfloat16)

        @pl.when(mine == r)
        def _():
            stat_ref[:, columns] = keep_share * prev_ref[:, columns] + scaled

        if c > r:
            low_ref[columns, rows] = low.T.astype(jnp.bfloat16)

            @pl.when(mine == c)
            def _():
                stat_ref[:, rows] = keep_share * prev_ref[:, rows] + scaled.T

    def own(k):
        return part_ref[k].astype(jnp.float32)

    def pass_right(k):
        rightward(k, to_right).wait_recv()
        to_right[k] = (own(k) + from_left[k].astype(jnp.float32)).astype(jnp.bfloat16)
        rightward(k, to_right).start()

    def pass_left(k):
        leftward(k, to_left).wait_recv()
        to_left[k] = (own(k) + from_right[k].astype(jnp.float32)).astype(jnp.bfloat16)
        leftward(k, to_left).start()

    def finish(k):
        emit(k, own(k) + from_left[k].astype(jnp.float32) + from_right[k].astype(jnp.float32))

    count = len(pairs)

    @pl.when(mine == 0)
    def _():
        for k in range(count):
            leftward(k, to_left).wait_recv()
            emit(k, own(k) + from_right[k].astype(jnp.float32))

    @pl.when(mine == last)
    def _():
        for k in range(count):
            rightward(k, to_right).wait_recv()
            emit(k, own(k) + from_left[k].astype(jnp.float32))

    lag = 2
    for near, far, here in (
        (pass_right, pass_left, (mine > 0) & (2 * mine < last)),
        (pass_left, pass_right, (mine < last) & (2 * mine >= last)),
    ):

        @pl.when(here)
        def _():
            for step in range(count + lag):
                if step < count:
                    near(step)
                if step >= lag:
                    far(step - lag)
                    finish(step - lag)

    for k in range(count):

        @pl.when(mine < last)
        def _():
            rightward(k, to_right).wait_send()

        @pl.when(mine > 0)
        def _():
            leftward(k, to_left).wait_send()


def chain_sum(part, full, prev_rows, share, groups):
    count, side = part.shape[0], part.shape[1]
    vmem = pl.BlockSpec(memory_space=pltpu.VMEM)
    dma = pltpu.SemaphoreType.DMA
    return pl.pallas_call(
        functools.partial(chain_kernel, groups, share),
        out_shape=(
            jax.ShapeDtypeStruct((groups * side, groups * side), jnp.bfloat16),
            jax.ShapeDtypeStruct(prev_rows.shape, jnp.float32),
        ),
        in_specs=[vmem] * 3,
        out_specs=(vmem, vmem),
        scratch_shapes=[pltpu.VMEM(part.shape, part.dtype)] * 4 + [dma((count,))] * 4,
        compiler_params=pltpu.CompilerParams(
            collective_id=1, has_side_effects=True, vmem_limit_bytes=40 << 20
        ),
    )(part, full, prev_rows)


def root_kernel(
    groups, owners, owner_ref, low_ref, full_hbm, grad_hbm, stat_hbm, rows_ref, update_hbm, new_hbm,
    stat_ref, grad_ref, factor, moment, square, fourth, root, result, sems,
):
    mine = lax.axis_index("group")
    order = low_ref.shape[0]
    side = order // groups
    fetch = pltpu.make_async_copy(grad_hbm, grad_ref, sems.at[0])
    fetch.start()
    take = pltpu.make_async_copy(stat_hbm, stat_ref, sems.at[2 + groups])
    take.start()
    live = owner_ref[lax.axis_index("expert")] < owners
    take.wait()
    give = pltpu.make_async_copy(stat_ref, new_hbm, sems.at[3 + groups])
    give.start()

    @pl.when(live)
    def _():
        vector = jnp.full((16, order), 1.0 / math.sqrt(order), jnp.float32)
        length = jnp.ones((1, 1), jnp.float32)
        for turn_index in range(POWER):
            image = jnp.dot(
                vector.astype(jnp.bfloat16), low_ref[...], preferred_element_type=jnp.float32
            )
            first = image[:1]
            length = jnp.sqrt(jnp.sum(first * first, axis=1, keepdims=True))
            vector = image / length
        scaling = 2.5 / length
        outer = jnp.sqrt(jnp.sqrt(scaling))

        def tile(t):
            return pl.ds(pl.multiple_of(t * side, side), side)

        def factor_of(t, value):
            row = lax.broadcasted_iota(jnp.int32, (side, order), 0) + t * side
            column = lax.broadcasted_iota(jnp.int32, (side, order), 1)
            identity = (row == column).astype(jnp.float32)
            return ((5.0 * identity - value) * 0.25).astype(jnp.bfloat16)

        def product(left, right, t):
            return jnp.dot(left[tile(t), :], right[...], preferred_element_type=jnp.float32)

        @pl.loop(0, groups)
        def _(t):
            value = scaling * low_ref[tile(t), :].astype(jnp.float32)
            moment[tile(t), :] = value.astype(jnp.bfloat16)
            factor[tile(t), :] = factor_of(t, value)

        @pl.loop(0, groups)
        def _(t):
            square[tile(t), :] = product(factor, factor, t).astype(jnp.bfloat16)

        @pl.loop(0, groups)
        def _(t):
            fourth[tile(t), :] = product(square, square, t).astype(jnp.bfloat16)

        @pl.loop(0, groups)
        def _(t):
            root[tile(t), :] = factor_of(t, product(fourth, moment, t))

        @pl.loop(0, groups)
        def _(t):
            square[tile(t), :] = (outer * product(factor, root, t)).astype(jnp.bfloat16)

    @pl.when(jnp.logical_not(live))
    def _():
        prior = pltpu.make_async_copy(full_hbm, square, sems.at[1])
        prior.start()
        prior.wait()

    rows_ref[...] = square[pl.ds(pl.multiple_of(mine * side, side), side), :]
    fetch.wait()
    tall = grad_ref.shape[0] // groups
    sends = []
    for t in range(groups):
        part = slice(t * tall, (t + 1) * tall)
        result[part, :] = jnp.dot(
            grad_ref[part, :], square[...], preferred_element_type=jnp.float32
        ).astype(jnp.bfloat16)
        sends.append(
            pltpu.make_async_copy(result.at[part, :], update_hbm.at[part, :], sems.at[2 + t])
        )
        sends[-1].start()
    for send in sends:
        send.wait()
    give.wait()


def finish_roots(owner_map, low, full, grad, stat, groups, owners):
    order = low.shape[0]
    vmem = pl.BlockSpec(memory_space=pltpu.VMEM)
    anywhere = pl.BlockSpec(memory_space=pl.ANY)
    square = pltpu.VMEM((order, order), jnp.bfloat16)
    tall = pltpu.VMEM(grad.shape, jnp.bfloat16)
    return pl.pallas_call(
        functools.partial(root_kernel, groups, owners),
        out_shape=(
            jax.ShapeDtypeStruct((order // groups, order), jnp.bfloat16),
            jax.ShapeDtypeStruct(grad.shape, jnp.bfloat16),
            jax.ShapeDtypeStruct(stat.shape, jnp.float32),
        ),
        in_specs=[pl.BlockSpec(memory_space=pltpu.SMEM), vmem] + [anywhere] * 3,
        out_specs=(vmem, anywhere, anywhere),
        scratch_shapes=[
            pltpu.VMEM(stat.shape, jnp.float32), tall, square, square, square, square, square, tall,
            pltpu.SemaphoreType.DMA((4 + groups,)),
        ],
    )(owner_map, low, full, grad, stat)


def body(tokens, cotangent, routing, stat_prev, root_prev, owner_map):
    expert_count = lax.axis_size("expert")
    group_count = lax.axis_size("group")
    tok_rows = tokens.shape[0]
    width_part = tokens.shape[1]
    hidden = cotangent.shape[1]
    row_block = stat_prev.shape[1]
    capacity = 2 * tok_rows // expert_count
    owners = expert_count // 4
    send_tokens, send_signal, payload = prepare(
        owner_map, routing, tokens, cotangent, stat_prev[0], root_prev[0],
        expert_count, capacity, owners,
    )
    send_tokens = send_tokens.reshape(expert_count, capacity, width_part)
    send_signal = send_signal.reshape(expert_count, capacity, hidden)
    got_tokens, got_signal, full = exchange(
        send_tokens, send_signal, payload, expert_count, group_count
    )
    got_tokens = got_tokens.reshape(expert_count * capacity, width_part)
    got_signal = got_signal.reshape(expert_count * capacity, hidden)
    grad = lax.dot_general(
        got_tokens, got_signal, (((0,), (0,)), ((), ())), preferred_element_type=jnp.float32
    )
    grad = (grad * (1.0 / math.sqrt(tok_rows))).astype(jnp.bfloat16)
    parts = []
    for r in range(group_count):
        panel = lax.dot_general(
            grad[:, r * row_block : (r + 1) * row_block],
            grad[:, r * row_block :],
            (((0,), (0,)), ((), ())),
            preferred_element_type=jnp.float32,
        ).astype(jnp.bfloat16)
        for c in range(group_count - r):
            parts.append(panel[:, c * row_block : (c + 1) * row_block])
    share = (1.0 - keep_share) / (width_part * group_count)
    stat_low, stat_new = chain_sum(jnp.stack(parts), full, stat_prev[0], share, group_count)
    root_rows, update, stat_new = finish_roots(
        owner_map, stat_low, full.reshape(hidden, hidden), grad, stat_new, group_count, owners
    )
    return (stat_new[None], root_rows[None], update[None])


def solution(mesh):
    in_specs = (
        P("expert", "group"),
        P("expert", None),
        P("expert", None),
        P("expert", "group", None),
        P("expert", "group", None),
        P(),
    )
    out_specs = (P("expert", "group", None), P("expert", "group", None), P("expert", "group", None))
    return jax.shard_map(body, mesh=mesh, in_specs=in_specs, out_specs=out_specs, check_vma=False)
```

```python
import functools
import math

import jax
import jax.numpy as jnp
from jax import lax
from jax.experimental import pallas as pl
from jax.experimental.pallas import tpu as pltpu
from jax.sharding import PartitionSpec as P

ITERS = 2
POWER = 8
MESH = pl.DeviceIdType.MESH

keep_share = 0.9


def prepare_kernel(
    capacity, owners, pieces, owner_ref, tall_ref, wide_ref, tok_ref, sig_ref, prev_ref, old_ref,
    tok_hbm, sig_hbm, pay_hbm, tok_out, sig_out, pay_out, sems,
):
    tok_rows = tok_ref.shape[0]
    live = owner_ref[lax.axis_index("expert")] < owners
    pay_out[...] = jnp.where(live, prev_ref[...].astype(jnp.bfloat16), old_ref[...])
    sends = [pltpu.make_async_copy(pay_out, pay_hbm, sems.at[2 * pieces])]
    sends[0].start()
    wide = wide_ref[...]
    before = lax.broadcasted_iota(jnp.int32, (tok_rows, tok_rows), 0)
    after = lax.broadcasted_iota(jnp.int32, (tok_rows, tok_rows), 1)
    earlier = jnp.where((tall_ref[...] == wide) & (before < after), 1, 0)
    column = wide * capacity + jnp.sum(earlier, axis=0, keepdims=True)
    piece = tok_out.shape[0] // pieces
    for t in range(pieces):
        rows = slice(t * piece, (t + 1) * piece)
        slots = lax.broadcasted_iota(jnp.int32, (piece, tok_rows), 0) + t * piece
        select = (slots == column).astype(jnp.float32).astype(jnp.bfloat16)
        for which, (src, out, hbm) in enumerate(
            ((tok_ref, tok_out, tok_hbm), (sig_ref, sig_out, sig_hbm))
        ):
            out[rows, :] = jnp.dot(
                select, src[...], preferred_element_type=jnp.float32
            ).astype(jnp.bfloat16)
            sends.append(
                pltpu.make_async_copy(
                    out.at[rows, :], hbm.at[rows, :], sems.at[2 * t + which]
                )
            )
            sends[-1].start()
    for send in sends:
        send.wait()


def prepare(owner_map, routing, tokens, cotangent, prev_rows, old_rows, experts, capacity, owners):
    slots = experts * capacity
    pieces = 4 if slots % 64 == 0 else 1
    vmem = pl.BlockSpec(memory_space=pltpu.VMEM)
    anywhere = pl.BlockSpec(memory_space=pl.ANY)
    shapes = (
        (slots, tokens.shape[1]), (slots, cotangent.shape[1]), prev_rows.shape,
    )
    return pl.pallas_call(
        functools.partial(prepare_kernel, capacity, owners, pieces),
        out_shape=tuple(jax.ShapeDtypeStruct(shape, jnp.bfloat16) for shape in shapes),
        in_specs=[pl.BlockSpec(memory_space=pltpu.SMEM)] + [vmem] * 6,
        out_specs=(anywhere,) * 3,
        scratch_shapes=[pltpu.VMEM(shape, jnp.bfloat16) for shape in shapes]
        + [pltpu.SemaphoreType.DMA((2 * pieces + 1,))],
    )(owner_map, routing, routing.reshape(1, -1), tokens, cotangent, prev_rows, old_rows)


def exchange_kernel(
    experts, groups, tok_ref, sig_ref, pay_ref, got_tok, got_sig, full,
    hold_tok, hold_sig, hold_pay, tok_send, tok_recv, sig_send, sig_recv, pay_send, pay_recv, own_sem,
):
    me = lax.axis_index("expert")
    mine = lax.axis_index("group")
    barrier = pltpu.get_barrier_semaphore()
    for d in range(1, experts):
        pl.semaphore_signal(
            barrier, inc=1, device_id={"expert": lax.rem(me + d, experts)}, device_id_type=MESH
        )
    for d in (1, groups - 1):
        pl.semaphore_signal(
            barrier, inc=1, device_id={"group": lax.rem(mine + d, groups)}, device_id_type=MESH
        )
    pl.semaphore_wait(barrier, experts + 1)
    last = groups - 1

    def relay(d, step, src):
        origin = lax.rem(mine + (groups - d) * step, groups)
        return pltpu.make_async_remote_copy(
            src_ref=full.at[origin] if src is None else src,
            dst_ref=full.at[origin],
            send_sem=pay_send.at[0 if d == 1 else 1, step],
            recv_sem=pay_recv.at[0 if d == 1 else 1, step],
            device_id={"group": lax.rem(mine + d, groups)},
            device_id_type=MESH,
        )

    @pl.when(mine < last)
    def _():
        relay(1, 0, pay_ref).start()

    @pl.when(mine > 0)
    def _():
        relay(last, 0, pay_ref).start()

    copies = []
    for d in range(1, experts):
        peer = lax.rem(me + d, experts)
        for src, dst, ssem, rsem in (
            (tok_ref, got_tok, tok_send, tok_recv),
            (sig_ref, got_sig, sig_send, sig_recv),
        ):
            copies.append(
                pltpu.make_async_remote_copy(
                    src_ref=src.at[peer],
                    dst_ref=dst.at[me],
                    send_sem=ssem.at[d],
                    recv_sem=rsem.at[d],
                    device_id={"expert": peer},
                    device_id_type=MESH,
                )
            )
    for copy in copies:
        copy.start()
    inward = (
        pltpu.make_async_copy(tok_ref.at[me], hold_tok, own_sem.at[0]),
        pltpu.make_async_copy(sig_ref.at[me], hold_sig, own_sem.at[1]),
        pltpu.make_async_copy(pay_ref, hold_pay, own_sem.at[2]),
    )
    for copy in inward:
        copy.start()
    for copy in inward:
        copy.wait()
    outward = (
        pltpu.make_async_copy(hold_tok, got_tok.at[me], own_sem.at[3]),
        pltpu.make_async_copy(hold_sig, got_sig.at[me], own_sem.at[4]),
        pltpu.make_async_copy(hold_pay, full.at[mine], own_sem.at[5]),
    )
    for copy in outward:
        copy.start()
    for copy in outward:
        copy.wait()
    for step in range(last):

        @pl.when(mine > step)
        def _():
            relay(1, step, None).wait_recv()

        @pl.when((mine > step) & (mine < last))
        def _():
            relay(1, step + 1, None).start()

        @pl.when(last - mine > step)
        def _():
            relay(last, step, None).wait_recv()

        @pl.when((last - mine > step) & (mine > 0))
        def _():
            relay(last, step + 1, None).start()

    for step in range(groups):

        @pl.when((mine >= step) & (mine < last))
        def _():
            relay(1, step, None).wait_send()

        @pl.when((last - mine >= step) & (mine > 0))
        def _():
            relay(last, step, None).wait_send()

    for copy in copies:
        copy.wait()


def exchange(send_tokens, send_signal, payload, experts, groups):
    anywhere = pl.BlockSpec(memory_space=pl.ANY)
    dma = pltpu.SemaphoreType.DMA
    return pl.pallas_call(
        functools.partial(exchange_kernel, experts, groups),
        out_shape=(
            jax.ShapeDtypeStruct(send_tokens.shape, send_tokens.dtype),
            jax.ShapeDtypeStruct(send_signal.shape, send_signal.dtype),
            jax.ShapeDtypeStruct((groups,) + payload.shape, payload.dtype),
        ),
        in_specs=[anywhere] * 3,
        out_specs=(anywhere,) * 3,
        scratch_shapes=[
            pltpu.VMEM(send_tokens.shape[1:], send_tokens.dtype),
            pltpu.VMEM(send_signal.shape[1:], send_signal.dtype),
            pltpu.VMEM(payload.shape, payload.dtype),
            dma((experts,)), dma((experts,)), dma((experts,)), dma((experts,)),
            dma((2, groups)), dma((2, groups)), dma((6,)),
        ],
        compiler_params=pltpu.CompilerParams(collective_id=0, has_side_effects=True),
    )(send_tokens, send_signal, payload)


def chain_kernel(
    groups, share, part_ref, full_ref, prev_ref, low_ref, stat_ref,
    from_left, from_right, to_right, to_left, right_send, right_recv, left_send, left_recv,
):
    mine = lax.axis_index("group")
    last = groups - 1
    side = part_ref.shape[1]
    barrier = pltpu.get_barrier_semaphore()

    for shift in (1, last):
        pl.semaphore_signal(
            barrier, inc=1, device_id={"group": lax.rem(mine + shift, groups)}, device_id_type=MESH
        )
    pl.semaphore_wait(barrier, 2)

    def rightward(k, src):
        return pltpu.make_async_remote_copy(
            src_ref=src.at[k],
            dst_ref=from_left.at[k],
            send_sem=right_send.at[k],
            recv_sem=right_recv.at[k],
            device_id={"group": lax.rem(mine + 1, groups)},
            device_id_type=MESH,
        )

    def leftward(k, src):
        return pltpu.make_async_remote_copy(
            src_ref=src.at[k],
            dst_ref=from_right.at[k],
            send_sem=left_send.at[k],
            recv_sem=left_recv.at[k],
            device_id={"group": lax.rem(mine + last, groups)},
            device_id_type=MESH,
        )

    pairs = [(r, c) for r in range(groups) for c in range(r, groups)]

    @pl.when(mine == 0)
    def _():
        for k in range(len(pairs)):
            rightward(k, part_ref).start()

    @pl.when(mine == last)
    def _():
        for k in range(len(pairs)):
            leftward(k, part_ref).start()

    def emit(k, total):
        r, c = pairs[k]
        rows, columns = slice(r * side, (r + 1) * side), slice(c * side, (c + 1) * side)
        scaled = share * total
        low = keep_share * full_ref[r, :, columns].astype(jnp.float32) + scaled
        low_ref[rows, columns] = low.astype(jnp.bfloat16)

        @pl.when(mine == r)
        def _():
            stat_ref[:, columns] = keep_share * prev_ref[:, columns] + scaled

        if c > r:
            low_ref[columns, rows] = low.T.astype(jnp.bfloat16)

            @pl.when(mine == c)
            def _():
                stat_ref[:, rows] = keep_share * prev_ref[:, rows] + scaled.T

    def own(k):
        return part_ref[k].astype(jnp.float32)

    def pass_right(k):
        rightward(k, to_right).wait_recv()
        to_right[k] = (own(k) + from_left[k].astype(jnp.float32)).astype(jnp.bfloat16)
        rightward(k, to_right).start()

    def pass_left(k):
        leftward(k, to_left).wait_recv()
        to_left[k] = (own(k) + from_right[k].astype(jnp.float32)).astype(jnp.bfloat16)
        leftward(k, to_left).start()

    def finish(k):
        emit(k, own(k) + from_left[k].astype(jnp.float32) + from_right[k].astype(jnp.float32))

    count = len(pairs)

    @pl.when(mine == 0)
    def _():
        for k in range(count):
            leftward(k, to_left).wait_recv()
            emit(k, own(k) + from_right[k].astype(jnp.float32))

    @pl.when(mine == last)
    def _():
        for k in range(count):
            rightward(k, to_right).wait_recv()
            emit(k, own(k) + from_left[k].astype(jnp.float32))

    lag = 2
    for near, far, here in (
        (pass_right, pass_left, (mine > 0) & (2 * mine < last)),
        (pass_left, pass_right, (mine < last) & (2 * mine >= last)),
    ):

        @pl.when(here)
        def _():
            for step in range(count + lag):
                if step < count:
                    near(step)
                if step >= lag:
                    far(step - lag)
                    finish(step - lag)

    for k in range(count):

        @pl.when(mine < last)
        def _():
            rightward(k, to_right).wait_send()

        @pl.when(mine > 0)
        def _():
            leftward(k, to_left).wait_send()


def chain_sum(part, full, prev_rows, share, groups):
    count, side = part.shape[0], part.shape[1]
    vmem = pl.BlockSpec(memory_space=pltpu.VMEM)
    dma = pltpu.SemaphoreType.DMA
    return pl.pallas_call(
        functools.partial(chain_kernel, groups, share),
        out_shape=(
            jax.ShapeDtypeStruct((groups * side, groups * side), jnp.bfloat16),
            jax.ShapeDtypeStruct(prev_rows.shape, jnp.float32),
        ),
        in_specs=[vmem] * 3,
        out_specs=(vmem, vmem),
        scratch_shapes=[pltpu.VMEM(part.shape, part.dtype)] * 4 + [dma((count,))] * 4,
        compiler_params=pltpu.CompilerParams(
            collective_id=1, has_side_effects=True, vmem_limit_bytes=40 << 20
        ),
    )(part, full, prev_rows)


def root_kernel(
    groups, owners, owner_ref, low_ref, full_hbm, grad_hbm, stat_hbm, rows_ref, update_hbm, new_hbm,
    stat_ref, grad_ref, factor, moment, square, fourth, root, result, sems,
):
    mine = lax.axis_index("group")
    order = low_ref.shape[0]
    side = order // groups
    fetch = pltpu.make_async_copy(grad_hbm, grad_ref, sems.at[0])
    fetch.start()
    take = pltpu.make_async_copy(stat_hbm, stat_ref, sems.at[2 + groups])
    take.start()
    live = owner_ref[lax.axis_index("expert")] < owners
    take.wait()
    give = pltpu.make_async_copy(stat_ref, new_hbm, sems.at[3 + groups])
    give.start()

    @pl.when(live)
    def _():
        vector = jnp.full((16, order), 1.0 / math.sqrt(order), jnp.float32)
        length = jnp.ones((1, 1), jnp.float32)
        for turn_index in range(POWER):
            image = jnp.dot(
                vector.astype(jnp.bfloat16), low_ref[...], preferred_element_type=jnp.float32
            )
            first = image[:1]
            length = jnp.sqrt(jnp.sum(first * first, axis=1, keepdims=True))
            vector = image / length
        scaling = 2.5 / length
        outer = jnp.sqrt(jnp.sqrt(scaling))

        def tile(t):
            return pl.ds(pl.multiple_of(t * side, side), side)

        def factor_of(t, value):
            row = lax.broadcasted_iota(jnp.int32, (side, order), 0) + t * side
            column = lax.broadcasted_iota(jnp.int32, (side, order), 1)
            identity = (row == column).astype(jnp.float32)
            return ((5.0 * identity - value) * 0.25).astype(jnp.bfloat16)

        def product(left, right, t):
            return jnp.dot(left[tile(t), :], right[...], preferred_element_type=jnp.float32)

        @pl.loop(0, groups)
        def _(t):
            value = scaling * low_ref[tile(t), :].astype(jnp.float32)
            moment[tile(t), :] = value.astype(jnp.bfloat16)
            factor[tile(t), :] = factor_of(t, value)

        @pl.loop(0, groups)
        def _(t):
            square[tile(t), :] = product(factor, factor, t).astype(jnp.bfloat16)

        @pl.loop(0, groups)
        def _(t):
            fourth[tile(t), :] = product(square, square, t).astype(jnp.bfloat16)

        @pl.loop(0, groups)
        def _(t):
            root[tile(t), :] = factor_of(t, product(fourth, moment, t))

        @pl.loop(0, groups)
        def _(t):
            square[tile(t), :] = (outer * product(factor, root, t)).astype(jnp.bfloat16)

    @pl.when(jnp.logical_not(live))
    def _():
        prior = pltpu.make_async_copy(full_hbm, square, sems.at[1])
        prior.start()
        prior.wait()

    rows_ref[...] = square[pl.ds(pl.multiple_of(mine * side, side), side), :]
    fetch.wait()
    tall = grad_ref.shape[0] // groups
    sends = []
    for t in range(groups):
        part = slice(t * tall, (t + 1) * tall)
        result[part, :] = jnp.dot(
            grad_ref[part, :], square[...], preferred_element_type=jnp.float32
        ).astype(jnp.bfloat16)
        sends.append(
            pltpu.make_async_copy(result.at[part, :], update_hbm.at[part, :], sems.at[2 + t])
        )
        sends[-1].start()
    for send in sends:
        send.wait()
    give.wait()


def finish_roots(owner_map, low, full, grad, stat, groups, owners):
    order = low.shape[0]
    vmem = pl.BlockSpec(memory_space=pltpu.VMEM)
    anywhere = pl.BlockSpec(memory_space=pl.ANY)
    square = pltpu.VMEM((order, order), jnp.bfloat16)
    tall = pltpu.VMEM(grad.shape, jnp.bfloat16)
    return pl.pallas_call(
        functools.partial(root_kernel, groups, owners),
        out_shape=(
            jax.ShapeDtypeStruct((order // groups, order), jnp.bfloat16),
            jax.ShapeDtypeStruct(grad.shape, jnp.bfloat16),
            jax.ShapeDtypeStruct(stat.shape, jnp.float32),
        ),
        in_specs=[pl.BlockSpec(memory_space=pltpu.SMEM), vmem] + [anywhere] * 3,
        out_specs=(vmem, anywhere, anywhere),
        scratch_shapes=[
            pltpu.VMEM(stat.shape, jnp.float32), tall, square, square, square, square, square, tall,
            pltpu.SemaphoreType.DMA((4 + groups,)),
        ],
        compiler_params=pltpu.CompilerParams(vmem_limit_bytes=40 << 20),
    )(owner_map, low, full, grad, stat)


def body(tokens, cotangent, routing, stat_prev, root_prev, owner_map):
    expert_count = lax.axis_size("expert")
    group_count = lax.axis_size("group")
    tok_rows = tokens.shape[0]
    width_part = tokens.shape[1]
    hidden = cotangent.shape[1]
    row_block = stat_prev.shape[1]
    capacity = 2 * tok_rows // expert_count
    owners = expert_count // 4
    send_tokens, send_signal, payload = prepare(
        owner_map, routing, tokens, cotangent, stat_prev[0], root_prev[0],
        expert_count, capacity, owners,
    )
    send_tokens = send_tokens.reshape(expert_count, capacity, width_part)
    send_signal = send_signal.reshape(expert_count, capacity, hidden)
    got_tokens, got_signal, full = exchange(
        send_tokens, send_signal, payload, expert_count, group_count
    )
    got_tokens = got_tokens.reshape(expert_count * capacity, width_part)
    got_signal = got_signal.reshape(expert_count * capacity, hidden)
    grad = lax.dot_general(
        got_tokens, got_signal, (((0,), (0,)), ((), ())), preferred_element_type=jnp.float32
    )
    grad = (grad * (1.0 / math.sqrt(tok_rows))).astype(jnp.bfloat16)
    parts = []
    for r in range(group_count):
        panel = lax.dot_general(
            grad[:, r * row_block : (r + 1) * row_block],
            grad[:, r * row_block :],
            (((0,), (0,)), ((), ())),
            preferred_element_type=jnp.float32,
        ).astype(jnp.bfloat16)
        for c in range(group_count - r):
            parts.append(panel[:, c * row_block : (c + 1) * row_block])
    share = (1.0 - keep_share) / (width_part * group_count)
    stat_low, stat_new = chain_sum(jnp.stack(parts), full, stat_prev[0], share, group_count)
    root_rows, update, stat_new = finish_roots(
        owner_map, stat_low, full.reshape(hidden, hidden), grad, stat_new, group_count, owners
    )
    return (stat_new[None], root_rows[None], update[None])


def solution(mesh):
    in_specs = (
        P("expert", "group"),
        P("expert", None),
        P("expert", None),
        P("expert", "group", None),
        P("expert", "group", None),
        P(),
    )
    out_specs = (P("expert", "group", None), P("expert", "group", None), P("expert", "group", None))
    return jax.shard_map(body, mesh=mesh, in_specs=in_specs, out_specs=out_specs, check_vma=False)
```
